32 devices in a mesh: tm: 4 (over y, core), expert: 8 (over z, x).
Axes of the slice: x: 2, y: 2, z: 4, core: 2. Of those that a mesh axis runs over, the one named last changes fastest.
Arguments:
- queries: bfloat16 [4096, 2048], P(('tm', 'expert')), may hold values from -6 to 6
- keys: bfloat16 [4096, 2048], P(('tm', 'expert')), may hold values from -6 to 6
- values: bfloat16 [4096, 2048], P(('tm', 'expert')), may hold values from -6 to 6
- out_grad: bfloat16 [4096, 2048], P(('tm', 'expert')), may hold values from -6 to 6
- expert_ids: int32 [4096, 2], P(('tm', 'expert')), may hold values from 0 to 7, all different within a row
- combine_gates: float32 [4096, 2], P(('tm', 'expert')), may hold values from 0.2 to 1
- gate_weight: bfloat16 [32, 2048, 512], P(('tm', 'expert')), may hold values from -0.125 to 0.125
- up_weight: bfloat16 [32, 2048, 512], P(('tm', 'expert')), may hold values from -0.125 to 0.125
- down_weight: bfloat16 [32, 512, 2048], P(('tm', 'expert')), may hold values from -0.125 to 0.125
Outputs:
- query_grad: bfloat16 [4096, 2048], P(('tm', 'expert'))
- key_grad: bfloat16 [4096, 2048], P(('tm', 'expert'))
- value_grad: bfloat16 [4096, 2048], P(('tm', 'expert'))
- gate_weight_grad: float32 [32, 2048, 512], P(('tm', 'expert'))
- up_weight_grad: float32 [32, 2048, 512], P(('tm', 'expert'))
- down_weight_grad: float32 [32, 512, 2048], P(('tm', 'expert'))
The draws below stay inside these ranges and needn't reach their ends.
Inputs may be any that keep to these rules, and one draw needn't show every extreme that they name: `expert_ids`: the two experts of a token differ.
All inputs are finite; a program needn't handle non-finite values.
Results may differ from the reference program's by a relative error of at most 0.017.
Values may be sent and summed in bfloat16 or wider, within the bound.
No kernel may reach another device: no remote copies, remote signals or barrier semaphores. Data moves between devices by JAX's collectives and lax.ppermute only.
A program may use at most 192 MiB of HBM per device.

```python
import jax
import jax.numpy as jnp
from jax import lax

HEADS = 16
HEAD_DIM = 128
D = 2048
FF = 2048
SLICES = 4
TOK_DEV = 128
EXPERTS = 8
CAP = 48
TOKENS = 4096
N_TM = 4
N_EXPERT = 8
DEVICES = 32


def level_of(stream_key, extent, pieces, smallest, top_value):
    def one(axis_at, shards_of):
        draws = jax.random.uniform(jax.random.fold_in(jax.random.fold_in(stream_key, 6), axis_at), (shards_of,), jnp.float32, smallest / len(pieces), top_value / len(pieces))
        return jnp.repeat(jnp.exp(draws), extent[axis_at] // shards_of).reshape((-1,) + (1,) * (len(extent) - axis_at - 1))

    level = one(*pieces[0])
    for cut in pieces[1:]:
        level = level * one(*cut)
    return level


def choose_distinct(rng, rows, amount, top, lift):
    order = jax.random.permutation(jax.random.fold_in(rng, 1), amount)
    pull = order
    for power in range(3):
        pull = pull * pull // amount
    pull = pull * lift // amount
    lots = jax.random.randint(jax.random.fold_in(rng, 2), (rows, amount), 0, 4096) + pull
    sure = jax.random.permutation(jax.random.fold_in(rng, 3), rows)[jnp.arange(amount) % rows]
    lots = jnp.where(jnp.arange(rows)[:, None] == sure[None, :], 1 << 14, lots)
    score = lots * amount + jnp.arange(amount)
    return lax.top_k(score.astype(jnp.int32), top)[1].astype(jnp.int32)


def gaussian(own_key, extent, scale, reach, split=(), kind=jnp.bfloat16):
    drawn = scale * jax.random.normal(own_key, extent, jnp.float32)
    if split:
        drawn = drawn * level_of(own_key, extent, split, -0.22, 0.18)
    return jnp.clip(drawn, -reach, reach).astype(kind)


def setup_inputs(seed: int = 0) -> dict:
    streams_of = jax.random.split(jax.random.key(seed), 10)
    queries = gaussian(streams_of[0], (TOKENS, D), 1.0, 6.0, ((0, 32),))
    keys = gaussian(streams_of[1], (TOKENS, D), 1.0, 6.0, ((0, 32),))
    values = gaussian(streams_of[2], (TOKENS, D), 1.0, 6.0, ((0, 32),))
    out_grad = gaussian(streams_of[3], (TOKENS, D), 1.0, 6.0, ((0, 32),))
    expert_ids = choose_distinct(streams_of[4], TOKENS, EXPERTS, 2, 4096)
    combine_gates = jnp.clip(0.2 + 0.8 * jax.random.uniform(streams_of[5], (TOKENS, 2), jnp.float32) ** level_of(streams_of[5], (TOKENS, 2), ((0, 32),), -0.2, 0.2), 0.2, 1.0)
    gate_weight = gaussian(streams_of[6], (EXPERTS * SLICES, D, FF // SLICES), D ** -0.5, 0.125, ((0, 32),))
    up_weight = gaussian(streams_of[7], (EXPERTS * SLICES, D, FF // SLICES), D ** -0.5, 0.125, ((0, 32),))
    down_weight = gaussian(streams_of[8], (EXPERTS * SLICES, FF // SLICES, D), FF ** -0.5, 0.125, ((0, 32),))
    return dict(queries=queries, keys=keys, values=values, out_grad=out_grad, expert_ids=expert_ids, combine_gates=combine_gates, gate_weight=gate_weight, up_weight=up_weight, down_weight=down_weight)


epsilon = 1e-06
highest = lax.Precision.HIGHEST

def slot_places(routes, capacity, experts):
    flat_ids = routes.reshape(-1).astype(jnp.int32)
    onehot = (flat_ids[:, None] == jnp.arange(experts, dtype=jnp.int32)[None, :]).astype(jnp.int32)
    earlier = jnp.cumsum(onehot, axis=0) - onehot
    position = lax.optimization_barrier(jnp.sum(earlier * onehot, axis=1))
    return jnp.where(position < capacity, flat_ids * capacity + position, experts * capacity).astype(jnp.int32)

def expert_slice(rows, grad_rows, gate_part, up_part, down_part):
    gate = jnp.dot(rows, gate_part, preferred_element_type=jnp.float32)
    upper = jnp.dot(rows, up_part, preferred_element_type=jnp.float32)
    sigma = jax.nn.sigmoid(gate)
    act = (gate * sigma * upper).astype(jnp.bfloat16)
    act_grad = jnp.dot(grad_rows, down_part.T, preferred_element_type=jnp.float32)
    down_grad = jnp.dot(act.T, grad_rows, preferred_element_type=jnp.float32)
    gate_grad = (act_grad * upper * sigma * (1.0 + gate * (1.0 - sigma))).astype(jnp.bfloat16)
    up_grad = (act_grad * gate * sigma).astype(jnp.bfloat16)
    gate_wgrad = jnp.dot(rows.T, gate_grad, preferred_element_type=jnp.float32)
    up_wgrad = jnp.dot(rows.T, up_grad, preferred_element_type=jnp.float32)
    partial_sum = jnp.dot(gate_grad, gate_part.T, preferred_element_type=jnp.float32)
    partial_sum = partial_sum + jnp.dot(up_grad, up_part.T, preferred_element_type=jnp.float32)
    return (partial_sum.astype(jnp.bfloat16), gate_wgrad, up_wgrad, down_grad)

def reference(queries, keys, values, out_grad, expert_ids, combine_gates, gate_weight, up_weight, down_weight):
    per_span = TOK_DEV * N_EXPERT
    shape4 = (N_TM, per_span, HEADS, HEAD_DIM)
    query_f = queries.astype(jnp.float32).reshape(shape4)
    key_f = keys.astype(jnp.float32).reshape(shape4)
    value_f = values.astype(jnp.float32).reshape(shape4)
    local = jnp.einsum('ctha,cthb->chab', key_f, value_f, precision=highest)
    states = jnp.cumsum(local, axis=0)
    mixed = jnp.einsum('ctha,chab->cthb', query_f, states, precision=highest)
    scale = lax.rsqrt(lax.optimization_barrier(jnp.mean(mixed * mixed, axis=-1, keepdims=True)) + epsilon)
    normed = mixed * scale
    hidden = normed.astype(jnp.bfloat16).reshape(TOKENS, D)
    routes = expert_ids.reshape(DEVICES, TOK_DEV, 2)
    places = jax.vmap(lambda route: slot_places(route, CAP, EXPERTS))(routes)
    rows_h = jnp.repeat(hidden.reshape(DEVICES, TOK_DEV, D), 2, axis=1)
    rows_g = jnp.repeat(out_grad.astype(jnp.float32).reshape(DEVICES, TOK_DEV, D), 2, axis=1)
    rows_g = (rows_g * combine_gates.reshape(DEVICES, 2 * TOK_DEV, 1)).astype(jnp.bfloat16)

    def fill_rows(place, rows):
        return jnp.zeros((EXPERTS * CAP, D), jnp.bfloat16).at[place].set(rows, mode='drop')
    buffer_h = jax.vmap(fill_rows)(places, rows_h).reshape(DEVICES, EXPERTS, CAP, D)
    buffer_g = jax.vmap(fill_rows)(places, rows_g).reshape(DEVICES, EXPERTS, CAP, D)
    token_index = (jnp.arange(DEVICES * 2 * TOK_DEV, dtype=jnp.int32) // 2).reshape(DEVICES, 2 * TOK_DEV)

    def fill_index(place, index_row):
        return jnp.full((EXPERTS * CAP,), TOKENS, jnp.int32).at[place].set(index_row, mode='drop')
    slot_token = jax.vmap(fill_index)(places, token_index).reshape(DEVICES, EXPERTS, CAP)
    width_slice = FF // SLICES
    gate_all = gate_weight.reshape(EXPERTS, SLICES, D, width_slice)
    up_all = up_weight.reshape(EXPERTS, SLICES, D, width_slice)
    down_all = down_weight.reshape(EXPERTS, SLICES, width_slice, D)

    def per_expert(carry, inputs):
        rows_in, grads_in, tokens_in, gate_e, up_e, down_e = inputs
        rows = rows_in.reshape(DEVICES * CAP, D)
        grad_rows = grads_in.reshape(DEVICES * CAP, D)
        total = jnp.zeros((DEVICES * CAP, D), jnp.float32)
        gate_list, up_list, down_list = ([], [], [])
        for slice_index in range(SLICES):
            partial_sum, gate_wgrad, up_wgrad, down_grad = expert_slice(rows, grad_rows, gate_e[slice_index], up_e[slice_index], down_e[slice_index])
            total = total + partial_sum.astype(jnp.float32)
            gate_list.append(gate_wgrad)
            up_list.append(up_wgrad)
            down_list.append(down_grad)
        carry = carry.at[tokens_in.reshape(-1)].add(total, mode='drop')
        return (carry, (jnp.stack(gate_list), jnp.stack(up_list), jnp.stack(down_list)))
    moe_grad, stacked = lax.scan(per_expert, jnp.zeros((TOKENS, D), jnp.float32), (jnp.transpose(buffer_h, (1, 0, 2, 3)), jnp.transpose(buffer_g, (1, 0, 2, 3)), jnp.transpose(slot_token, (1, 0, 2)), gate_all, up_all, down_all))
    gate_weight_grad = stacked[0].reshape(EXPERTS * SLICES, D, width_slice)
    up_weight_grad = stacked[1].reshape(EXPERTS * SLICES, D, width_slice)
    down_weight_grad = stacked[2].reshape(EXPERTS * SLICES, width_slice, D)
    hidden_grad = (out_grad.astype(jnp.float32) + moe_grad).reshape(shape4)
    norm_grad = scale * (hidden_grad - normed * lax.optimization_barrier(jnp.mean(hidden_grad * normed, axis=-1, keepdims=True)))
    query_grad = jnp.einsum('cthb,chab->ctha', norm_grad, states, precision=highest)
    local_back = jnp.einsum('ctha,cthb->chab', query_f, norm_grad, precision=highest)
    back_states = jnp.flip(jnp.cumsum(jnp.flip(local_back, 0), axis=0), 0)
    key_grad = jnp.einsum('cthb,chab->ctha', value_f, back_states, precision=highest)
    value_grad = jnp.einsum('ctha,chab->cthb', key_f, back_states, precision=highest)
    return (query_grad.reshape(TOKENS, D).astype(jnp.bfloat16), key_grad.reshape(TOKENS, D).astype(jnp.bfloat16), value_grad.reshape(TOKENS, D).astype(jnp.bfloat16), gate_weight_grad, up_weight_grad, down_weight_grad)
```

```python
import functools

import jax
import jax.numpy as jnp
from jax import lax
from jax.experimental import pallas as pl
from jax.experimental.pallas import tpu as pltpu
from jax.sharding import Mesh, PartitionSpec as P

HEADS = 16
HEAD_DIM = 128
SLICES = 4
EPSILON = 1e-06
ALL = ("tm", "eg", "sl")
F32 = jnp.float32
BF16 = jnp.bfloat16


def dot(a, b):
    return jnp.dot(a, b, preferred_element_type=F32)


def dot_nt(a, b):
    return lax.dot_general(a, b, (((1,), (1,)), ((), ())), preferred_element_type=F32)


def dot_tn(a, b):
    return lax.dot_general(a, b, (((0,), (0,)), ((), ())), preferred_element_type=F32)


def slot_places(routes, capacity, experts):
    flat_ids = routes.reshape(-1)
    onehot = (flat_ids[:, None] == jnp.arange(experts, dtype=jnp.int32)[None, :]).astype(jnp.int32)
    earlier = jnp.cumsum(onehot, axis=0) - onehot
    position = jnp.sum(earlier * onehot, axis=1)
    return jnp.where(position < capacity, flat_ids * capacity + position, experts * capacity)


def swap(value, bit):
    return lax.ppermute(value, "sl", [(i, i ^ bit) for i in range(SLICES)])


def exchange(value, axes):
    return lax.all_to_all(value, axes, split_axis=0, concat_axis=0, tiled=True)


def spread(rows):
    half = rows.shape[0] // 2
    a, b = rows[:half], rows[half:]
    ax, bz = swap(a, 1), swap(b, 2)
    az, bx = swap(a, 2), swap(b, 1)
    ad, bd = swap(ax, 2), swap(bz, 1)
    return (a, b), (ax, bx), (az, bz), (ad, bd)


def wgrad_kernel(count, *refs):
    xs, ys, acts, ggs, ugs = (refs[i * count : (i + 1) * count] for i in range(5))
    gate_out, up_out, down_out = refs[5 * count :]
    gate = up = down = None
    for x, y, act, gg, ug in zip(xs, ys, acts, ggs, ugs):
        g, u, d = dot_tn(x[...], gg[...]), dot_tn(x[...], ug[...]), dot_tn(act[...], y[...])
        gate = g if gate is None else gate + g
        up = u if up is None else up + u
        down = d if down is None else down + d
    gate_out[...], up_out[...], down_out[...] = gate, up, down


def weight_grads(xs, ys, acts, ggs, ugs):
    width = xs[0].shape[1]
    hidden = acts[0].shape[1]
    block = min(256, width)
    wide = [pl.BlockSpec((x.shape[0], block), lambda i: (0, i)) for x in xs]
    full = [pl.BlockSpec((x.shape[0], hidden), lambda i: (0, 0)) for x in xs]
    return pl.pallas_call(
        functools.partial(wgrad_kernel, len(xs)),
        grid=(width // block,),
        in_specs=wide + wide + full + full + full,
        out_specs=[
            pl.BlockSpec((block, hidden), lambda i: (i, 0)),
            pl.BlockSpec((block, hidden), lambda i: (i, 0)),
            pl.BlockSpec((hidden, block), lambda i: (0, i)),
        ],
        out_shape=[
            jax.ShapeDtypeStruct((width, hidden), F32),
            jax.ShapeDtypeStruct((width, hidden), F32),
            jax.ShapeDtypeStruct((hidden, width), F32),
        ],
        name="weight_grads",
    )(*xs, *ys, *acts, *ggs, *ugs)


def body(queries, keys, values, out_grad, expert_ids, combine_gates, gate_weight, up_weight, down_weight):
    tok_rows, width = queries.shape
    times, groups = lax.axis_size("tm"), lax.axis_size("eg")
    experts = times * groups
    devices = experts * SLICES
    per_span = groups * SLICES
    capacity = SLICES * max(1, 3 * tok_rows // (experts * SLICES))
    shape3 = (tok_rows, HEADS, HEAD_DIM)
    state_rows = HEADS * HEAD_DIM // devices
    gate_w, up_w, down_w = gate_weight[0], up_weight[0], down_weight[0]
    query3, key3, value3 = queries.reshape(shape3), keys.reshape(shape3), values.reshape(shape3)

    def span_sums(terms, backward):
        got = exchange(terms.astype(BF16).reshape(HEADS * HEAD_DIM, HEAD_DIM), ALL)
        got = got.reshape(times, per_span, state_rows, HEAD_DIM).astype(F32)
        spans = jnp.sum(got, axis=1)
        order = range(times - 1, -1, -1) if backward else range(times)
        total, sums = None, [None] * times
        for c in order:
            total = spans[c] if total is None else total + spans[c]
            sums[c] = total
        sums = jnp.stack(sums).astype(BF16)
        send = jnp.broadcast_to(sums[:, None], (times, per_span, state_rows, HEAD_DIM))
        back = exchange(send.reshape(devices * state_rows, HEAD_DIM), ALL)
        return back.reshape(HEADS, HEAD_DIM, HEAD_DIM)

    places = slot_places(expert_ids, capacity, experts).reshape(tok_rows, 2)
    slots = jnp.arange(experts * capacity, dtype=jnp.int32)
    pick = [(slots[:, None] == places[None, :, k]).astype(BF16) for k in range(2)]
    pick_both = jnp.concatenate(pick, axis=1)
    pick_token = pick[0] + pick[1]

    local = jnp.einsum("tha,thb->hab", key3, value3, preferred_element_type=F32)
    states = span_sums(local, False)

    grad_f = out_grad.astype(F32)
    scaled = jnp.concatenate([(grad_f * combine_gates[:, k : k + 1]).astype(BF16) for k in range(2)])
    slot_g = dot(pick_both, scaled).astype(BF16)
    grads = spread(exchange(slot_g, ("tm", "eg")))

    mixed = jnp.einsum("tha,hab->thb", query3, states, preferred_element_type=F32)
    scale = lax.rsqrt(jnp.mean(mixed * mixed, axis=-1, keepdims=True) + EPSILON)
    normed = mixed * scale
    hidden = normed.astype(BF16).reshape(tok_rows, width)
    slot_h = dot(pick_token, hidden).astype(BF16)
    rows = spread(exchange(slot_h, ("tm", "eg")))

    flat = lambda nested: [piece for pair in nested for piece in pair]
    xs, ys = flat(rows), flat(grads)
    acts, ggs, ugs, parts = [], [], [], []
    for x, y in zip(xs, ys):
        gate, upper = dot(x, gate_w), dot(x, up_w)
        sigma = jax.nn.sigmoid(gate)
        act_grad = dot_nt(y, down_w)
        acts.append((gate * sigma * upper).astype(BF16))
        gg = (act_grad * upper * sigma * (1.0 + gate * (1.0 - sigma))).astype(BF16)
        ug = (act_grad * gate * sigma).astype(BF16)
        ggs.append(gg)
        ugs.append(ug)
        parts.append(dot_nt(gg, gate_w) + dot_nt(ug, up_w))
    (oa, ob, xa, xb, za, zb, da, db) = parts
    da_in, db_in = swap(da.astype(BF16), 2), swap(db.astype(BF16), 1)
    za_in, xb_in = swap(za.astype(BF16), 2), swap(xb.astype(BF16), 1)
    xa_in = swap((xa + da_in.astype(F32)).astype(BF16), 1)
    zb_in = swap((zb + db_in.astype(F32)).astype(BF16), 2)
    own = jnp.concatenate(
        [
            (oa + za_in.astype(F32) + xa_in.astype(F32)).astype(BF16),
            (ob + xb_in.astype(F32) + zb_in.astype(F32)).astype(BF16),
        ]
    )
    gate_wgrad, up_wgrad, down_grad = weight_grads(xs, ys, acts, ggs, ugs)
    returned = exchange(own, ("tm", "eg"))
    moe_grad = dot_tn(pick_token, returned)
    hidden_grad = (grad_f + moe_grad).reshape(shape3)
    norm_grad = scale * (hidden_grad - normed * jnp.mean(hidden_grad * normed, axis=-1, keepdims=True))
    norm_grad = norm_grad.astype(BF16)
    local_back = jnp.einsum("tha,thb->hab", query3, norm_grad, preferred_element_type=F32)
    back_states = span_sums(local_back, True)
    query_grad = jnp.einsum("thb,hab->tha", norm_grad, states, preferred_element_type=F32)
    key_grad = jnp.einsum("thb,hab->tha", value3, back_states, preferred_element_type=F32)
    value_grad = jnp.einsum("tha,hab->thb", key3, back_states, preferred_element_type=F32)
    return (
        query_grad.reshape(tok_rows, width).astype(BF16),
        key_grad.reshape(tok_rows, width).astype(BF16),
        value_grad.reshape(tok_rows, width).astype(BF16),
        gate_wgrad[None],
        up_wgrad[None],
        down_grad[None],
    )


def solution(mesh):
    times, members = mesh.devices.shape
    fine = Mesh(mesh.devices.reshape(times, members // SLICES, SLICES), ALL)
    two, three = P(ALL, None), P(ALL, None, None)
    return jax.shard_map(
        body,
        mesh=fine,
        in_specs=(two,) * 6 + (three,) * 3,
        out_specs=(two,) * 3 + (three,) * 3,
        check_vma=False,
    )
```

```python
import functools

import jax
import jax.numpy as jnp
from jax import lax
from jax.experimental import pallas as pl
from jax.sharding import Mesh, PartitionSpec as P


HEAD_DIM = 128
SLICES = 4
EPSILON = 1e-06
ALL = ("tm", "eg", "sl")
F32 = jnp.float32
BF16 = jnp.bfloat16


def dot(a, b):
    return jnp.dot(a, b, preferred_element_type=F32)


def dot_nt(a, b):
    return lax.dot_general(a, b, (((1,), (1,)), ((), ())), preferred_element_type=F32)


def dot_tn(a, b):
    return lax.dot_general(a, b, (((0,), (0,)), ((), ())), preferred_element_type=F32)


def call(kernel, out_shape, *args, **options):
    return pl.pallas_call(kernel, out_shape=out_shape, **options)(*args)


def like(shape, dtype=BF16):
    return jax.ShapeDtypeStruct(shape, dtype)


def head_cols(h):
    return slice(h * HEAD_DIM, (h + 1) * HEAD_DIM)


def swap(value, bit):
    return lax.ppermute(value, "sl", [(i, i ^ bit) for i in range(SLICES)])


def exchange(value, axes):
    return lax.all_to_all(value, axes, split_axis=0, concat_axis=0, tiled=True)


def trade(blocks):
    count = len(blocks)
    moved = list(blocks)
    for k in range(1, count):
        moved[k] = lax.ppermute(blocks[k], ("tm", "eg"), [(i, i ^ k) for i in range(count)])
    return moved


def spread(rows, first):
    other = 3 - first
    one, two = swap(rows, first), swap(rows, other)
    far = swap(one, other)
    return {0: rows, first: one, other: two, 3: far}


def join_kernel(*refs):
    out = refs[-1]
    rows = refs[0].shape[0]
    for i, ref in enumerate(refs[:-1]):
        out[i * rows : (i + 1) * rows] = ref[...]


def join(blocks):
    rows, width = blocks[0].shape
    if rows % 16:
        return jnp.concatenate(blocks)
    return call(join_kernel, like((len(blocks) * rows, width)), *blocks)


def slot_places(routes, capacity, experts):
    flat_ids = routes.reshape(-1)
    onehot = (flat_ids[:, None] == jnp.arange(experts, dtype=jnp.int32)[None, :]).astype(jnp.int32)
    earlier = jnp.cumsum(onehot, axis=0) - onehot
    position = jnp.sum(earlier * onehot, axis=1)
    return jnp.where(position < capacity, flat_ids * capacity + position, experts * capacity)


def pick(places, choice, block, rows):
    slots = block * rows + lax.broadcasted_iota(jnp.int32, (rows, places.shape[1]), 0)
    return slots == places[choice : choice + 1]


def one_hot(mask):
    return jnp.where(mask, 1.0, 0.0).astype(BF16)


def outer_kernel(keys, values, out):
    for h in range(keys.shape[1] // HEAD_DIM):
        cols = head_cols(h)
        out[cols] = dot_tn(keys[:, cols], values[:, cols]).astype(BF16)


def slots_kernel(groups, sources, scaled, *refs):
    infos, tokens, outs = refs[:sources], refs[sources : 2 * sources], refs[2 * sources :]
    rows = outs[0].shape[0] // sources
    for n in range(sources):
        info = infos[n][...]
        spots = info[:2].astype(jnp.int32)
        blocks = []
        for q in range(len(outs)):
            picks = [pick(spots, k, q * groups, rows) for k in range(2)]
            if scaled:
                blocks.append(jnp.concatenate([one_hot(p) for p in picks], axis=1))
            else:
                blocks.append(one_hot(picks[0] | picks[1]))
        if scaled:
            grad = tokens[n][...].astype(F32)
            gates = info.T
            values = jnp.concatenate([(grad * gates[:, 2 + k : 3 + k]).astype(BF16) for k in range(2)])
        else:
            values = tokens[n][...]
        if rows % 16:
            for block, out in zip(blocks, outs):
                out[n * rows : (n + 1) * rows] = dot(block, values).astype(BF16)
        else:
            chosen = dot(jnp.concatenate(blocks), values).astype(BF16)
            for q, out in enumerate(outs):
                out[n * rows : (n + 1) * rows] = chosen[q * rows : (q + 1) * rows]


def slots(infos, tokens, capacity, times, groups, scaled):
    sources, width = len(tokens), tokens[0].shape[1]
    return call(
        functools.partial(slots_kernel, groups, sources, scaled),
        [like((sources * capacity, width))] * times,
        *infos, *tokens,
    )


def hidden_kernel(queries, states, hidden):
    for h in range(queries.shape[1] // HEAD_DIM):
        cols = head_cols(h)
        mixed = dot(queries[:, cols], states[cols])
        scale = lax.rsqrt(jnp.mean(mixed * mixed, axis=-1, keepdims=True) + EPSILON)
        hidden[:, cols] = (mixed * scale).astype(BF16)


def act_grad_kernel(*refs):
    ys, down_w, out = refs[:-2], refs[-2], refs[-1]
    out[...] = dot_nt(jnp.concatenate([y[...] for y in ys]), down_w[...])


def act_grads(ys, down_w):
    rows = sum(y.shape[0] for y in ys)
    return call(act_grad_kernel, like((rows, down_w.shape[0]), F32), *ys, down_w)


def expert_kernel(pieces, regroup, *refs):
    xs, (act_grad, gate_w, up_w, act_out, gg_out, ug_out), parts = refs[:pieces], refs[pieces : pieces + 6], refs[pieces + 6 :]
    x = jnp.concatenate([x[...] for x in xs])
    gate, upper, grad = dot(x, gate_w[...]), dot(x, up_w[...]), act_grad[...]
    sigma = jax.nn.sigmoid(gate)
    silu = gate * sigma
    act_out[...] = (silu * upper).astype(BF16)
    gg = (grad * upper * sigma * (1.0 + gate * (1.0 - sigma))).astype(BF16)
    ug = (grad * silu).astype(BF16)
    gg_out[...], ug_out[...] = gg, ug
    rows, width = parts[0].shape
    count = x.shape[0] // rows
    for j in range(len(parts) // count):
        cols = slice(j * width, (j + 1) * width)
        total = (dot_nt(gg, gate_w[cols]) + dot_nt(ug, up_w[cols])).astype(BF16)
        if regroup:
            block = rows // pieces
            for m in range(count):
                for q in range(pieces):
                    at = (q * count + m) * block
                    parts[count * j + m][q * block : (q + 1) * block] = total[at : at + block]
        else:
            for m in range(count):
                parts[count * j + m][...] = total[m * rows : (m + 1) * rows]


def expert_rows(xs, act_grad, gate_w, up_w, halves, count, regroup):
    total, width = sum(x.shape[0] for x in xs), xs[0].shape[1]
    hidden = gate_w.shape[1]
    outs = call(
        functools.partial(expert_kernel, len(xs), regroup),
        [like((total, hidden))] * 3 + [like((total // count, width // halves))] * (count * halves),
        *xs, act_grad, gate_w, up_w,
    )
    parts = [[outs[3 + count * j + m] for j in range(halves)] for m in range(count)]
    return outs[0], outs[1], outs[2], parts


def sum_kernel(count, *refs):
    total = refs[0][...].astype(F32)
    for ref in refs[1:count]:
        total = total + ref[...].astype(F32)
    outs = refs[count:]
    rows = outs[0].shape[0]
    if rows % 16 and len(outs) > 1:
        for n, out in enumerate(outs):
            part = refs[0][n * rows : (n + 1) * rows].astype(F32)
            for ref in refs[1:count]:
                part = part + ref[n * rows : (n + 1) * rows].astype(F32)
            out[...] = part.astype(BF16)
    else:
        total = total.astype(BF16)
        for n, out in enumerate(outs):
            out[...] = total[n * rows : (n + 1) * rows]


def add_up(pieces, count=1):
    rows, width = pieces[0].shape
    outs = call(functools.partial(sum_kernel, len(pieces)), [like((rows // count, width))] * count, *pieces)
    return outs[0] if count == 1 else outs


def wgrad_kernel(turned, count, *refs):
    rows, cols, out = refs[:count], refs[count:-1], refs[-1]
    left = jnp.concatenate([r[...] for r in rows])
    right = jnp.concatenate([c[...] for c in cols])
    out[...] = dot_tn(right, left) if turned else dot_tn(left, right)


def weight_grad(wide, narrow, turned):
    width, hidden = wide[0].shape[1], narrow[0].shape[1]
    block = min(1024, width)
    shape = (1, hidden, width) if turned else (1, width, hidden)
    out = (None, hidden, block) if turned else (None, block, hidden)
    return call(
        functools.partial(wgrad_kernel, turned, len(wide)),
        like(shape, F32),
        *wide, *narrow,
        grid=(width // block,),
        in_specs=[pl.BlockSpec((w.shape[0], block), lambda i: (0, i)) for w in wide]
        + [pl.BlockSpec(n.shape, lambda i: (0, 0)) for n in narrow],
        out_specs=pl.BlockSpec(out, (lambda i: (0, 0, i)) if turned else (lambda i: (0, i, 0))),
    )


def norm_kernel(places, queries, states, out_grad, *refs):
    blocks, local_back, norm_out = refs[:-2], refs[-2], refs[-1]
    spots = places[...]
    rows = blocks[0].shape[0]
    picks = [one_hot(pick(spots, 0, n, rows) | pick(spots, 1, n, rows)) for n in range(len(blocks))]
    if rows % 16:
        moe = dot_tn(picks[0], blocks[0][...])
        for chosen, block in zip(picks[1:], blocks[1:]):
            moe = moe + dot_tn(chosen, block[...])
    else:
        moe = dot_tn(jnp.concatenate(picks), jnp.concatenate([block[...] for block in blocks]))
    hidden_grads = out_grad[...].astype(F32) + moe
    for h in range(queries.shape[1] // HEAD_DIM):
        cols = head_cols(h)
        query, state = queries[:, cols], states[cols]
        mixed = dot(query, state)
        scale = lax.rsqrt(jnp.mean(mixed * mixed, axis=-1, keepdims=True) + EPSILON)
        normed = mixed * scale
        hidden_grad = hidden_grads[:, cols]
        norm_grad = scale * (hidden_grad - normed * jnp.mean(hidden_grad * normed, axis=-1, keepdims=True))
        norm_grad = norm_grad.astype(BF16)
        norm_out[:, cols] = norm_grad
        local_back[cols] = dot_tn(query, norm_grad).astype(BF16)


def query_kernel(norm_grad, states, query_grad):
    for h in range(norm_grad.shape[1] // HEAD_DIM):
        cols = head_cols(h)
        query_grad[:, cols] = dot_nt(norm_grad[:, cols], states[cols]).astype(BF16)


def key_kernel(keys, values, back, key_grad, value_grad):
    for h in range(keys.shape[1] // HEAD_DIM):
        cols = head_cols(h)
        state = back[cols]
        key_grad[:, cols] = dot_nt(values[:, cols], state).astype(BF16)
        value_grad[:, cols] = dot(keys[:, cols], state).astype(BF16)


def body(queries, keys, values, out_grad, expert_ids, combine_gates, gate_weight, up_weight, down_weight):
    tok_rows, width = queries.shape
    times, groups = lax.axis_size("tm"), lax.axis_size("eg")
    experts = times * groups
    devices = experts * SLICES
    per_span = groups * SLICES
    capacity = SLICES * max(1, 3 * tok_rows // (experts * SLICES))
    halves = 1
    first_g, first_h, first_back = (2, 1), (2, 2), (2, 2)
    others = range(1, groups)

    def to_owners(terms):
        return exchange(terms, ALL)

    def span_sums(got, backward):
        rows = got.shape[0] // devices
        got = got.reshape(times, per_span, rows, HEAD_DIM).astype(F32)
        spans = jnp.sum(got, axis=1)
        order = range(times - 1, -1, -1) if backward else range(times)
        total, sums = None, [None] * times
        for c in order:
            total = spans[c] if total is None else total + spans[c]
            sums[c] = total
        sums = jnp.stack(sums).astype(BF16)
        send = jnp.broadcast_to(sums[:, None], (times, per_span, rows, HEAD_DIM))
        return send.reshape(devices * rows, HEAD_DIM)

    me = lax.axis_index("tm") * groups + lax.axis_index("eg")
    ids = expert_ids.T
    spots = slot_places(expert_ids, capacity, experts).reshape(tok_rows, 2).T
    kept = spots < experts * capacity
    position = jnp.where(kept, spots - ids * capacity, -1)
    info = jnp.concatenate([ids.astype(F32), position.astype(F32), combine_gates.T, jnp.zeros((2, tok_rows), F32)])

    def localize(info):
        ids, position = info[:2].astype(jnp.int32), info[2:4].astype(jnp.int32)
        places = jnp.where(position < 0, -1, (ids ^ me) * capacity + position)
        return jnp.concatenate([places.astype(F32), info[4:6], jnp.zeros((4, tok_rows), F32)])

    def from_group(value, f):
        return lax.ppermute(value, "eg", [(i, i ^ f) for i in range(groups)])

    own_info = localize(info)
    places = own_info[:2].astype(jnp.int32)
    near_infos = [own_info] + [localize(swap(info, s)) for s in range(1, SLICES)]
    far_infos = [None] + [localize(from_group(info, f)) for f in others]

    def trade_times(blocks):
        moved = list(blocks)
        for q in range(1, times):
            moved[q] = lax.ppermute(blocks[q], "tm", [(i, i ^ q) for i in range(times)])
        return moved

    def dispatch(tokens, firsts, scaled):
        far_tokens = [from_group(tokens, f) for f in others]
        square = spread(tokens, firsts[0])
        far = []
        for f, other in zip(others, far_tokens):
            blocks = slots([far_infos[f]], [other], capacity, times, groups, scaled)
            blocks = trade_times(blocks)
            far.append(spread(join(blocks), firsts[1]))
        near = slots(near_infos, [square[s] for s in range(SLICES)], capacity, times, groups, scaled)
        return trade_times(near), far

    terms = call(outer_kernel, like((width, HEAD_DIM)), keys, values)
    got_terms = to_owners(terms)
    near_g, far_g = dispatch(out_grad, first_g, True)
    states = exchange(span_sums(got_terms, False), ALL)
    hidden = call(hidden_kernel, like((tok_rows, width)), queries, states)
    near_h, far_h = dispatch(hidden, first_h, False)

    gate_w, up_w, down_w = gate_weight[0], up_weight[0], down_weight[0]
    xs, ys, acts, ggs, ugs, parts = [], [], [], [], [], {}

    def expert(x, y, keys_, regroup=False):
        grads = act_grads(y, down_w)
        act, gg, ug, part = expert_rows(x, grads, gate_w, up_w, halves, len(keys_), regroup)
        for key, pair in zip(keys_, part):
            parts[key] = pair
        xs.extend(x)
        ys.extend(y)
        acts.append(act)
        ggs.append(gg)
        ugs.append(ug)

    expert(near_h, near_g, [(0, s) for s in range(SLICES)], True)
    for f in others:
        x, y = far_h[f - 1], far_g[f - 1]
        for group in ((0, 1, 2), (3,)):
            expert([x[s] for s in group], [y[s] for s in group], [(f, s) for s in group])

    returns = []
    for j in range(halves):
        blocks = [None] * experts
        for p in range(groups):
            first = first_back[p > 0]
            other = 3 - first
            far_in = swap(parts[p, 3][j], other)
            own_in = swap(parts[p, other][j], other)
            mid = add_up([parts[p, first][j], far_in])
            mid_in = swap(mid, first)
            total = add_up([parts[p, 0][j], own_in, mid_in], times)
            for q in range(times):
                blocks[q * groups + p] = total[q]
        returns.append(trade(blocks))

    gate_wgrad = weight_grad(xs, ggs, False)
    up_wgrad = weight_grad(xs, ugs, False)
    down_wgrad = weight_grad(ys, acts, True)

    local_back, norm_grad = call(
        norm_kernel, [like((width, HEAD_DIM)), like((tok_rows, width))],
        places, queries, states, out_grad, *returns[0],
    )
    query_grad = call(query_kernel, like((tok_rows, width)), norm_grad, states)
    sums = span_sums(to_owners(local_back), True)
    back = exchange(sums, ALL)
    key_grad, value_grad = call(key_kernel, [like(keys.shape)] * 2, keys, values, back)
    return query_grad, key_grad, value_grad, gate_wgrad, up_wgrad, down_wgrad


def solution(mesh):
    times, members = mesh.devices.shape
    fine = Mesh(mesh.devices.reshape(times, members // SLICES, SLICES), ALL)
    two, three = P(ALL, None), P(ALL, None, None)
    return jax.shard_map(
        body,
        mesh=fine,
        in_specs=(two,) * 6 + (three,) * 3,
        out_specs=(two,) * 3 + (three,) * 3,
        check_vma=False,
    )
```

```python
import functools

import jax
import jax.numpy as jnp
from jax import lax
from jax.experimental import pallas as pl
from jax.sharding import Mesh, PartitionSpec as P


HEAD_DIM = 128
SLICES = 4
EPSILON = 1e-06
ALL = ("tm", "eg", "sl")
F32 = jnp.float32
BF16 = jnp.bfloat16


def dot(a, b):
    return jnp.dot(a, b, preferred_element_type=F32)


def dot_nt(a, b):
    return lax.dot_general(a, b, (((1,), (1,)), ((), ())), preferred_element_type=F32)


def dot_tn(a, b):
    return lax.dot_general(a, b, (((0,), (0,)), ((), ())), preferred_element_type=F32)


def call(kernel, out_shape, *args, **options):
    return pl.pallas_call(kernel, out_shape=out_shape, **options)(*args)


def like(shape, dtype=BF16):
    return jax.ShapeDtypeStruct(shape, dtype)


def head_cols(h):
    return slice(h * HEAD_DIM, (h + 1) * HEAD_DIM)


def swap(value, bit):
    return lax.ppermute(value, "sl", [(i, i ^ bit) for i in range(SLICES)])


def exchange(value, axes):
    return lax.all_to_all(value, axes, split_axis=0, concat_axis=0, tiled=True)


def trade(blocks):
    count = len(blocks)
    moved = list(blocks)
    for k in range(1, count):
        moved[k] = lax.ppermute(blocks[k], ("tm", "eg"), [(i, i ^ k) for i in range(count)])
    return moved


def spread(rows, first):
    other = 3 - first
    one, two = swap(rows, first), swap(rows, other)
    far = swap(one, other)
    return {0: rows, first: one, other: two, 3: far}


def join_kernel(*refs):
    out = refs[-1]
    rows = refs[0].shape[0]
    for i, ref in enumerate(refs[:-1]):
        out[i * rows : (i + 1) * rows] = ref[...]


def join(blocks):
    rows, width = blocks[0].shape
    if rows % 16:
        return jnp.concatenate(blocks)
    return call(join_kernel, like((len(blocks) * rows, width)), *blocks)


def slot_places(routes, capacity, experts):
    flat_ids = routes.reshape(-1)
    onehot = (flat_ids[:, None] == jnp.arange(experts, dtype=jnp.int32)[None, :]).astype(jnp.int32)
    earlier = jnp.cumsum(onehot, axis=0) - onehot
    position = jnp.sum(earlier * onehot, axis=1)
    return jnp.where(position < capacity, flat_ids * capacity + position, experts * capacity)


def pick(places, choice, block, rows):
    slots = block * rows + lax.broadcasted_iota(jnp.int32, (rows, places.shape[1]), 0)
    return slots == places[choice : choice + 1]


def one_hot(mask):
    return jnp.where(mask, 1.0, 0.0).astype(BF16)


def outer_kernel(keys, values, out):
    for h in range(keys.shape[1] // HEAD_DIM):
        cols = head_cols(h)
        out[cols] = dot_tn(keys[:, cols], values[:, cols]).astype(BF16)


def slots_kernel(groups, sources, scaled, *refs):
    infos, tokens, outs = refs[:sources], refs[sources : 2 * sources], refs[2 * sources :]
    rows = outs[0].shape[0] // sources
    for n in range(sources):
        info = infos[n][...]
        spots = info[:2].astype(jnp.int32)
        blocks = []
        for q in range(len(outs)):
            picks = [pick(spots, k, q * groups, rows) for k in range(2)]
            if scaled:
                blocks.append(jnp.concatenate([one_hot(p) for p in picks], axis=1))
            else:
                blocks.append(one_hot(picks[0] | picks[1]))
        if scaled:
            grad = tokens[n][...].astype(F32)
            gates = info.T
            values = jnp.concatenate([(grad * gates[:, 2 + k : 3 + k]).astype(BF16) for k in range(2)])
        else:
            values = tokens[n][...]
        if rows % 16:
            for block, out in zip(blocks, outs):
                out[n * rows : (n + 1) * rows] = dot(block, values).astype(BF16)
        else:
            chosen = dot(jnp.concatenate(blocks), values).astype(BF16)
            for q, out in enumerate(outs):
                out[n * rows : (n + 1) * rows] = chosen[q * rows : (q + 1) * rows]


def slots(infos, tokens, capacity, times, groups, scaled):
    sources, width = len(tokens), tokens[0].shape[1]
    return call(
        functools.partial(slots_kernel, groups, sources, scaled),
        [like((sources * capacity, width))] * times,
        *infos, *tokens,
    )


def hidden_kernel(queries, states, hidden):
    for h in range(queries.shape[1] // HEAD_DIM):
        cols = head_cols(h)
        mixed = dot(queries[:, cols], states[cols])
        scale = lax.rsqrt(jnp.mean(mixed * mixed, axis=-1, keepdims=True) + EPSILON)
        hidden[:, cols] = (mixed * scale).astype(BF16)


def act_grad_kernel(*refs):
    ys, down_w, out = refs[:-2], refs[-2], refs[-1]
    out[...] = dot_nt(jnp.concatenate([y[...] for y in ys]), down_w[...])


def act_grads(ys, down_w):
    rows = sum(y.shape[0] for y in ys)
    return call(act_grad_kernel, like((rows, down_w.shape[0]), F32), *ys, down_w)


def expert_kernel(pieces, regroup, *refs):
    xs, (act_grad, gate_w, up_w, act_out, gg_out, ug_out), parts = refs[:pieces], refs[pieces : pieces + 6], refs[pieces + 6 :]
    x = jnp.concatenate([x[...] for x in xs])
    gate, upper, grad = dot(x, gate_w[...]), dot(x, up_w[...]), act_grad[...]
    sigma = jax.nn.sigmoid(gate)
    silu = gate * sigma
    act_out[...] = (silu * upper).astype(BF16)
    gg = (grad * upper * sigma * (1.0 + gate * (1.0 - sigma))).astype(BF16)
    ug = (grad * silu).astype(BF16)
    gg_out[...], ug_out[...] = gg, ug
    rows, width = parts[0].shape
    count = x.shape[0] // rows
    for j in range(len(parts) // count):
        cols = slice(j * width, (j + 1) * width)
        total = (dot_nt(gg, gate_w[cols]) + dot_nt(ug, up_w[cols])).astype(BF16)
        if regroup:
            block = rows // pieces
            for m in range(count):
                for q in range(pieces):
                    at = (q * count + m) * block
                    parts[count * j + m][q * block : (q + 1) * block] = total[at : at + block]
        else:
            for m in range(count):
                parts[count * j + m][...] = total[m * rows : (m + 1) * rows]


def expert_rows(xs, act_grad, gate_w, up_w, halves, count, regroup):
    total, width = sum(x.shape[0] for x in xs), xs[0].shape[1]
    hidden = gate_w.shape[1]
    outs = call(
        functools.partial(expert_kernel, len(xs), regroup),
        [like((total, hidden))] * 3 + [like((total // count, width // halves))] * (count * halves),
        *xs, act_grad, gate_w, up_w,
    )
    parts = [[outs[3 + count * j + m] for j in range(halves)] for m in range(count)]
    return outs[0], outs[1], outs[2], parts


def sum_kernel(count, *refs):
    total = refs[0][...].astype(F32)
    for ref in refs[1:count]:
        total = total + ref[...].astype(F32)
    outs = refs[count:]
    rows = outs[0].shape[0]
    if rows % 16 and len(outs) > 1:
        for n, out in enumerate(outs):
            part = refs[0][n * rows : (n + 1) * rows].astype(F32)
            for ref in refs[1:count]:
                part = part + ref[n * rows : (n + 1) * rows].astype(F32)
            out[...] = part.astype(BF16)
    else:
        total = total.astype(BF16)
        for n, out in enumerate(outs):
            out[...] = total[n * rows : (n + 1) * rows]


def add_up(pieces, count=1):
    rows, width = pieces[0].shape
    outs = call(functools.partial(sum_kernel, len(pieces)), [like((rows // count, width))] * count, *pieces)
    return outs[0] if count == 1 else outs


def wgrad_kernel(turned, count, *refs):
    rows, cols, out = refs[:count], refs[count:-1], refs[-1]
    left = jnp.concatenate([r[...] for r in rows])
    right = jnp.concatenate([c[...] for c in cols])
    out[...] = dot_tn(right, left) if turned else dot_tn(left, right)


def weight_grad(wide, narrow, turned):
    width, hidden = wide[0].shape[1], narrow[0].shape[1]
    block = min(1024, width)
    shape = (1, hidden, width) if turned else (1, width, hidden)
    out = (None, hidden, block) if turned else (None, block, hidden)
    return call(
        functools.partial(wgrad_kernel, turned, len(wide)),
        like(shape, F32),
        *wide, *narrow,
        grid=(width // block,),
        in_specs=[pl.BlockSpec((w.shape[0], block), lambda i: (0, i)) for w in wide]
        + [pl.BlockSpec(n.shape, lambda i: (0, 0)) for n in narrow],
        out_specs=pl.BlockSpec(out, (lambda i: (0, 0, i)) if turned else (lambda i: (0, i, 0))),
    )


def norm_kernel(halves, places, queries, states, out_grad, *refs):
    blocks, local_back, norm_out = refs[:-2], refs[-2], refs[-1]
    spots = places[...]
    count = len(blocks) // halves
    rows = blocks[0].shape[0]
    picks = [one_hot(pick(spots, 0, n, rows) | pick(spots, 1, n, rows)) for n in range(count)]
    moe = []
    for j in range(halves):
        mine = blocks[j * count : (j + 1) * count]
        if rows % 16:
            part = dot_tn(picks[0], mine[0][...])
            for chosen, block in zip(picks[1:], mine[1:]):
                part = part + dot_tn(chosen, block[...])
        else:
            part = dot_tn(jnp.concatenate(picks), jnp.concatenate([block[...] for block in mine]))
        moe.append(part)
    hidden_grads = out_grad[...].astype(F32) + jnp.concatenate(moe, axis=1)
    for h in range(queries.shape[1] // HEAD_DIM):
        cols = head_cols(h)
        query, state = queries[:, cols], states[cols]
        mixed = dot(query, state)
        scale = lax.rsqrt(jnp.mean(mixed * mixed, axis=-1, keepdims=True) + EPSILON)
        normed = mixed * scale
        hidden_grad = hidden_grads[:, cols]
        norm_grad = scale * (hidden_grad - normed * jnp.mean(hidden_grad * normed, axis=-1, keepdims=True))
        norm_grad = norm_grad.astype(BF16)
        norm_out[:, cols] = norm_grad
        local_back[cols] = dot_tn(query, norm_grad).astype(BF16)


def query_kernel(norm_grad, states, query_grad):
    for h in range(norm_grad.shape[1] // HEAD_DIM):
        cols = head_cols(h)
        query_grad[:, cols] = dot_nt(norm_grad[:, cols], states[cols]).astype(BF16)


def key_kernel(keys, values, back, key_grad, value_grad):
    for h in range(keys.shape[1] // HEAD_DIM):
        cols = head_cols(h)
        state = back[cols]
        key_grad[:, cols] = dot_nt(values[:, cols], state).astype(BF16)
        value_grad[:, cols] = dot(keys[:, cols], state).astype(BF16)


def body(queries, keys, values, out_grad, expert_ids, combine_gates, gate_weight, up_weight, down_weight):
    tok_rows, width = queries.shape
    times, groups = lax.axis_size("tm"), lax.axis_size("eg")
    experts = times * groups
    devices = experts * SLICES
    per_span = groups * SLICES
    capacity = SLICES * max(1, 3 * tok_rows // (experts * SLICES))
    halves = 2
    first_g, first_h, first_back = (2, 1), (2, 2), ((1, 2), (2, 2))
    others = range(1, groups)

    def to_owners(terms):
        return exchange(terms, ALL)

    def span_sums(got, backward):
        rows = got.shape[0] // devices
        got = got.reshape(times, per_span, rows, HEAD_DIM).astype(F32)
        spans = jnp.sum(got, axis=1)
        order = range(times - 1, -1, -1) if backward else range(times)
        total, sums = None, [None] * times
        for c in order:
            total = spans[c] if total is None else total + spans[c]
            sums[c] = total
        sums = jnp.stack(sums).astype(BF16)
        send = jnp.broadcast_to(sums[:, None], (times, per_span, rows, HEAD_DIM))
        return send.reshape(devices * rows, HEAD_DIM)

    me = lax.axis_index("tm") * groups + lax.axis_index("eg")
    ids = expert_ids.T
    spots = slot_places(expert_ids, capacity, experts).reshape(tok_rows, 2).T
    kept = spots < experts * capacity
    position = jnp.where(kept, spots - ids * capacity, -1)
    info = jnp.concatenate([ids.astype(F32), position.astype(F32), combine_gates.T, jnp.zeros((2, tok_rows), F32)])

    def localize(info):
        ids, position = info[:2].astype(jnp.int32), info[2:4].astype(jnp.int32)
        places = jnp.where(position < 0, -1, (ids ^ me) * capacity + position)
        return jnp.concatenate([places.astype(F32), info[4:6], jnp.zeros((4, tok_rows), F32)])

    def from_group(value, f):
        return lax.ppermute(value, "eg", [(i, i ^ f) for i in range(groups)])

    own_info = localize(info)
    places = own_info[:2].astype(jnp.int32)
    near_infos = [own_info] + [localize(swap(info, s)) for s in range(1, SLICES)]
    far_infos = [None] + [localize(from_group(info, f)) for f in others]

    def trade_times(blocks):
        moved = list(blocks)
        for q in range(1, times):
            moved[q] = lax.ppermute(blocks[q], "tm", [(i, i ^ q) for i in range(times)])
        return moved

    def dispatch(tokens, firsts, scaled):
        far_tokens = [from_group(tokens, f) for f in others]
        square = spread(tokens, firsts[0])
        far = []
        for f, other in zip(others, far_tokens):
            blocks = slots([far_infos[f]], [other], capacity, times, groups, scaled)
            blocks = trade_times(blocks)
            far.append(spread(join(blocks), firsts[1]))
        near = slots(near_infos, [square[s] for s in range(SLICES)], capacity, times, groups, scaled)
        return trade_times(near), far

    terms = call(outer_kernel, like((width, HEAD_DIM)), keys, values)
    got_terms = to_owners(terms)
    near_g, far_g = dispatch(out_grad, first_g, True)
    states = exchange(span_sums(got_terms, False), ALL)
    hidden = call(hidden_kernel, like((tok_rows, width)), queries, states)
    near_h, far_h = dispatch(hidden, first_h, False)

    gate_w, up_w, down_w = gate_weight[0], up_weight[0], down_weight[0]
    xs, ys, acts, ggs, ugs, parts = [], [], [], [], [], {}

    def expert(x, y, keys_, regroup=False):
        grads = act_grads(y, down_w)
        act, gg, ug, part = expert_rows(x, grads, gate_w, up_w, halves, len(keys_), regroup)
        for key, pair in zip(keys_, part):
            parts[key] = pair
        xs.extend(x)
        ys.extend(y)
        acts.append(act)
        ggs.append(gg)
        ugs.append(ug)

    expert(near_h, near_g, [(0, s) for s in range(SLICES)], True)
    for f in others:
        x, y = far_h[f - 1], far_g[f - 1]
        for group in ((0, 1, 2), (3,)):
            expert([x[s] for s in group], [y[s] for s in group], [(f, s) for s in group])

    returns = []
    for j in range(halves):
        blocks = [None] * experts
        for p in range(groups):
            first = first_back[j][p > 0]
            other = 3 - first
            far_in = swap(parts[p, 3][j], other)
            own_in = swap(parts[p, other][j], other)
            mid = add_up([parts[p, first][j], far_in])
            mid_in = swap(mid, first)
            total = add_up([parts[p, 0][j], own_in, mid_in], times)
            for q in range(times):
                blocks[q * groups + p] = total[q]
        returns.append(trade(blocks))

    gate_wgrad = weight_grad(xs, ggs, False)
    up_wgrad = weight_grad(xs, ugs, False)
    down_wgrad = weight_grad(ys, acts, True)

    local_back, norm_grad = call(
        functools.partial(norm_kernel, halves), [like((width, HEAD_DIM)), like((tok_rows, width))],
        places, queries, states, out_grad, *sum(returns, []),
    )
    query_grad = call(query_kernel, like((tok_rows, width)), norm_grad, states)
    sums = span_sums(to_owners(local_back), True)
    back = exchange(sums, ALL)
    key_grad, value_grad = call(key_kernel, [like(keys.shape)] * 2, keys, values, back)
    return query_grad, key_grad, value_grad, gate_wgrad, up_wgrad, down_wgrad


def solution(mesh):
    times, members = mesh.devices.shape
    fine = Mesh(mesh.devices.reshape(times, members // SLICES, SLICES), ALL)
    two, three = P(ALL, None), P(ALL, None, None)
    return jax.shard_map(
        body,
        mesh=fine,
        in_specs=(two,) * 6 + (three,) * 3,
        out_specs=(two,) * 3 + (three,) * 3,
        check_vma=False,
    )
```
